256 devices in a mesh: group: 4 (over x), dp: 2 (over y_lo), tensor: 32 (over y_hi, z, core).
Axes of the slice: x: 4, y: 4 (y_hi: 2, y_lo: 2; y = y_hi * 2 + y_lo), z: 8, core: 2. Of those that a mesh axis runs over, the one named last changes fastest.
Arguments:
- weight: float32 [14848, 8192], P('group', ('dp', 'tensor')), may hold values from -0.046875 to 0.046875
- moment: float32 [14848, 8192], P('group', ('dp', 'tensor')), may hold values from -1.8 to 1.8
- second: float32 [14848, 8192], P('group', ('dp', 'tensor')), may hold values from 0.02 to 0.3
- gradient: bfloat16 [14848, 8192], P('group', ('dp', 'tensor')), may hold values from -600 to 600
- hidden: bfloat16 [1024, 14848], P(('group', 'dp'), 'tensor'), may hold values from -6 to 6
- stream: bfloat16 [1024, 8192], P(('group', 'dp'), 'tensor'), may hold values from -32 to 32
- norm_gain: bfloat16 [8192], P('tensor'), may hold values from 0.25 to 1.75
Outputs:
- weight_new: float32 [14848, 8192], P('group', ('dp', 'tensor'))
- moment_new: float32 [14848, 8192], P('group', ('dp', 'tensor'))
- second_new: float32 [14848, 8192], P('group', ('dp', 'tensor'))
- normed: bfloat16 [1024, 8192], P(('group', 'dp'), 'tensor')
- residual: bfloat16 [1024, 8192], P(('group', 'dp'), 'tensor')
The draws below stay inside these ranges and needn't reach their ends.
All inputs are finite; a program needn't handle non-finite values.
Results may differ from the reference program's by a relative error of at most 0.0095.
Values may be sent and summed in bfloat16 or wider, within the bound.
No kernel may reach another device: no remote copies, remote signals or barrier semaphores. Data moves between devices by JAX's collectives and lax.ppermute only.
A program may use at most 64 MiB of HBM per device.

```python
import math
import jax
import jax.numpy as jnp
from jax import lax

D = 8192
FFW = 14848
ROWS = 128
TOTAL_ROWS = 1024
N_GROUP = 4
N_DP = 2
N_TENSOR = 32


def draw_gradient(key, part):
    row_pos = jnp.arange(FFW, dtype=jnp.float32)[:, None] / FFW
    col_pos = jnp.arange(D, dtype=jnp.float32)[None, :] / D
    rising = jnp.exp(0.5 * jnp.log(3.0) * (row_pos + col_pos))
    values = jax.random.truncated_normal(key, -4.0, 4.0, (FFW, D), jnp.float32) * rising
    return values.astype(jnp.bfloat16)


def draw_stream(key, part):
    total_rows = ROWS * N_GROUP * N_DP
    col_pos = jnp.arange(D, dtype=jnp.float32)[None, :] / D
    key_base = jax.random.fold_in(jax.random.fold_in(key, 7), 0)
    rising = jnp.exp(jnp.log(3.0) * col_pos)
    values = jax.random.truncated_normal(key_base, -4.0, 4.0, (total_rows, D), jnp.float32) * rising
    return values.astype(jnp.bfloat16)


def block_scale(key, shape, cuts, least, high):
    gain, own = 1.0, jax.random.fold_in(key, 6)
    for dim, blocks in cuts:
        draws = jnp.exp(jax.random.uniform(jax.random.fold_in(own, dim), (blocks,), jnp.float32, least / len(cuts), high / len(cuts)))
        gain = gain * jnp.repeat(draws, shape[dim] // blocks).reshape([-1 if axis == dim else 1 for axis in range(len(shape))])
    return gain


def gaussian(rng, dims, deviation, limit, pieces=(), kind=jnp.bfloat16):
    drawn = jax.random.normal(rng, dims, jnp.float32) * deviation
    if len(pieces) > 0:
        drawn = block_scale(rng, dims, pieces, -0.22, 0.18) * drawn
    return jnp.clip(drawn, min=-limit, max=limit).astype(kind)


def setup_inputs(seed: int = 0) -> dict:
    seeds = jax.random.split(jax.random.key(seed), 8)
    return {
        "weight": gaussian(seeds[0], (FFW, D), FFW ** -0.5, 0.046875, ((0, 4), (1, 64)), jnp.float32),
        "moment": gaussian(seeds[1], (FFW, D), 0.3, 1.8, ((0, 4), (1, 64)), jnp.float32),
        "second": jnp.clip(jnp.exp(math.log(0.3) - 2.7080503 * jax.random.uniform(seeds[2], (FFW, D), jnp.float32) ** block_scale(seeds[2], (FFW, D), ((0, 4), (1, 64)), -0.2, 0.2)), 0.02, 0.3),
        "gradient": draw_gradient(jax.random.fold_in(seeds[7], 71), 0),
        "hidden": gaussian(seeds[4], (TOTAL_ROWS, FFW), 1.0, 6.0, ((0, 8), (1, 32))),
        "stream": draw_stream(jax.random.fold_in(seeds[7], 71), 0),
        "norm_gain": jnp.clip(1.0 + 0.15 * jax.random.normal(seeds[6], (D,), jnp.float32), 0.25, 1.75).astype(jnp.bfloat16),
    }


clip_rms = 0.5
beta_one = 0.9
beta_two = 0.95
bias_one = 1.0 - 0.9 ** 10
bias_two = 1.0 - 0.95 ** 10
adam_eps = 1e-08
learn_rate = 0.002

def reference(weight, moment, second, gradient, hidden, stream, norm_gain):
    grad_float = gradient.astype(jnp.float32)
    grad_total = jnp.sum(grad_float * grad_float)
    factor = jnp.minimum(1.0, clip_rms * jnp.sqrt(jnp.float32(FFW * D)) / (jnp.sqrt(grad_total) + 1e-06))
    clipped = factor * grad_float
    moment_new = beta_one * moment + (1.0 - beta_one) * clipped
    second_new = beta_two * second + (1.0 - beta_two) * clipped * clipped
    update = moment_new / bias_one / (jnp.sqrt(second_new / bias_two) + adam_eps)
    weight_new = weight - learn_rate * update
    shipped = weight_new.astype(jnp.bfloat16)
    slice_rows = FFW // N_TENSOR

    def accumulate(running, block_index):
        hidden_part = lax.dynamic_slice_in_dim(hidden, block_index * slice_rows, slice_rows, 1)
        weight_part = lax.dynamic_slice_in_dim(shipped, block_index * slice_rows, slice_rows, 0)
        product = jnp.dot(hidden_part, weight_part, preferred_element_type=jnp.float32)
        rounded = lax.optimization_barrier(product.astype(jnp.bfloat16))
        return (running + rounded.astype(jnp.float32), None)
    empty_sum = jnp.zeros((hidden.shape[0], D), jnp.float32)
    summed, _ = lax.scan(accumulate, empty_sum, jnp.arange(N_TENSOR, dtype=jnp.int32))
    residual_sum = stream.astype(jnp.float32) + summed
    squares = lax.optimization_barrier(jnp.sum(residual_sum * residual_sum, axis=1, keepdims=True))
    normed = residual_sum * lax.rsqrt(squares / D + 1e-06) * norm_gain.astype(jnp.float32)
    return (weight_new, moment_new, second_new, normed.astype(jnp.bfloat16), residual_sum.astype(jnp.bfloat16))
```

```python
import functools
import math

import jax
import jax.numpy as jnp
from jax import lax
from jax.experimental import pallas as pl
from jax.experimental.pallas import tpu as pltpu
from jax.sharding import Mesh
from jax.sharding import PartitionSpec as P

D = 8192
FFW = 14848
AXES = ("g", "d", "h", "z", "c")
PLANE = ("d", "h", "z", "c")
SIZES = {"g": 4, "d": 2, "h": 2, "z": 8, "c": 2}
SLICE = 464
KA = 256
KB = SLICE - KA

clip_rms = 0.5
beta_one = 0.9
beta_two = 0.95
bias_one = 1.0 - 0.9**10
bias_two = 1.0 - 0.95**10
adam_eps = 1e-08
learn_rate = 0.002


def shift(x, axis, k):
    n = SIZES[axis]
    return lax.ppermute(x, axis, [(i, (i + k) % n) for i in range(n)])


def shift_y(x, k):
    pairs = []
    for d in range(2):
        for h in range(2):
            y = (h * 2 + d + k) % 4
            pairs.append((d * 2 + h, (y % 2) * 2 + y // 2))
    return lax.ppermute(x, ("d", "h"), pairs)


def hidden_pairs():
    pairs = []
    for g in range(4):
        for d in range(2):
            for h in range(2):
                for z in range(8):
                    for c in range(2):
                        src = (((g * 2 + d) * 2 + h) * 8 + z) * 2 + c
                        to = (h * 2 + z // 4, c, g // 2, (g % 2) * 4 + z % 4, d)
                        dst = (((to[0] * 2 + to[1]) * 2 + to[2]) * 8 + to[3]) * 2 + to[4]
                        pairs.append((src, dst))
    return pairs


def owner_pairs():
    pairs = []
    for d in range(2):
        for h in range(2):
            for z in range(8):
                for c in range(2):
                    src = ((d * 2 + h) * 8 + z) * 2 + c
                    dst = ((c * 2 + d) * 8 + h * 4 + z // 2) * 2 + z % 2
                    pairs.append((src, dst))
    return pairs


def gather_plane(mine):
    part_a, part_b = mine[:KA], mine[KA:]
    up, down = [part_a], [part_a]
    for _ in range(4):
        up.append(shift(up[-1], "z", 1))
    for _ in range(3):
        down.append(shift(down[-1], "z", -1))
    line = jnp.stack(up + down[1:])
    offsets = [0, 1, 2, 3, 4, -1, -2, -3]
    one = shift_y(line, 1)
    minus = shift_y(line, -1)
    two_a = shift_y(one[:4], 1)
    two_b = shift_y(minus[4:], -1)
    pieces = [
        (0, offsets, 0, line),
        (1, offsets, 0, one),
        (-1, offsets, 0, minus),
        (2, offsets[:4], 0, two_a),
        (2, offsets[4:], 0, two_b),
    ]
    column = jnp.stack([part_b, shift_y(part_b, 1), shift_y(part_b, -1), shift_y(part_b, 2)])
    y_offsets = [0, 1, -1, 2]
    up, down = [column], [column]
    for _ in range(3):
        up.append(shift(up[-1], "z", 1))
        down.append(shift(down[-1], "z", -1))
    four_a = shift(up[-1][:2], "z", 1)
    four_b = shift(down[-1][2:], "z", -1)
    pieces.append((y_offsets, 0, 1, column))
    for k in range(1, 4):
        pieces.append((y_offsets, k, 1, up[k]))
        pieces.append((y_offsets, -k, 1, down[k]))
    pieces.append((y_offsets[:2], 4, 1, four_a))
    pieces.append((y_offsets[2:], 4, 1, four_b))
    return pieces


def product(pieces, own, other):
    g, d, h, z, c = (lax.axis_index(a) for a in AXES)
    y = h * 2 + d
    wheres, owners, parts = [], [], []
    for ys, zs, part, array in pieces:
        pairs = [(ys, j) for j in zs] if isinstance(ys, int) else [(i, zs) for i in ys]
        for i, j in pairs:
            at_y, at_z = (y - i) % 4, (z - j) % 8
            wheres.append((at_z % 4 * 2 + at_y % 2) * SLICE + (0, KA)[part])
            owners.append((at_y // 2 * 2 + at_z // 4 - g) % 4)
        parts.append((part, len(pairs)))
    index = jnp.stack(wheres + owners + [c]).astype(jnp.int32)
    count = len(wheres)

    def kernel(index_ref, own_ref, other_ref, *refs):
        blocks = refs[: len(parts)]
        outs = refs[len(parts) : len(parts) + 4]
        total = refs[-1]
        total[...] = jnp.zeros_like(total)
        n = 0
        for (part, length), block in zip(parts, blocks):
            depth = (KA, KB)[part]
            for k in range(length):
                start = pl.multiple_of(index_ref[n], 16)
                owner = index_ref[count + n]
                rows = block[k]
                for side, ref in ((0, own_ref), (1, other_ref)):
                    total[owner, side] += lax.dot_general(
                        rows,
                        ref[pl.ds(start, depth), :],
                        (((0,), (0,)), ((), ())),
                        preferred_element_type=jnp.float32,
                    )
                n += 1
        core = index_ref[2 * count]
        for k in range(4):
            outs[k][:, pl.ds(pl.multiple_of(core * 128, 128), 128)] = total[k, 0].astype(
                jnp.bfloat16
            )
            outs[k][:, pl.ds(pl.multiple_of((1 - core) * 128, 128), 128)] = total[k, 1].astype(
                jnp.bfloat16
            )

    vmem = pl.BlockSpec(memory_space=pltpu.VMEM)
    return pl.pallas_call(
        kernel,
        out_shape=[jax.ShapeDtypeStruct((128, 256), jnp.bfloat16)] * 4,
        in_specs=[pl.BlockSpec(memory_space=pltpu.SMEM)] + [vmem] * (2 + len(pieces)),
        out_specs=[vmem] * 4,
        scratch_shapes=[pltpu.VMEM((4, 2, 128, 128), jnp.float32)],
        compiler_params=pltpu.CompilerParams(vmem_limit_bytes=24 * 1024 * 1024),
        cost_estimate=pl.CostEstimate(
            flops=2 * 512 * 3712 * 256, bytes_accessed=6_000_000, transcendentals=0
        ),
    )(index, own, other, *[array for _, _, _, array in pieces])


def per_device(weight, moment, second, gradient, hidden, stream, norm_gain):
    c = lax.axis_index("c")
    d = lax.axis_index("d")
    pieces = gather_plane(lax.ppermute(hidden.T, AXES, hidden_pairs()))
    from_owner = [(b, a) for a, b in owner_pairs()]
    stream_here = lax.ppermute(stream, PLANE, from_owner).astype(jnp.float32)

    grad_float = gradient.astype(jnp.float32)
    mine = jnp.sum(grad_float * grad_float, axis=0)
    spread = jnp.broadcast_to(mine[None, None], (256, 1, 128))
    grad_total = jnp.sum(lax.all_to_all(spread, AXES, split_axis=0, concat_axis=0, tiled=True))
    factor = jnp.minimum(1.0, clip_rms * math.sqrt(FFW * D) / (jnp.sqrt(grad_total) + 1e-06))
    clipped = factor * grad_float
    moment_new = beta_one * moment + (1.0 - beta_one) * clipped
    second_new = beta_two * second + (1.0 - beta_two) * clipped * clipped
    update = moment_new / bias_one / (jnp.sqrt(second_new / bias_two) + adam_eps)
    weight_new = weight - learn_rate * update
    shipped = weight_new.astype(jnp.bfloat16)

    sums = product(pieces, shipped, shift(shipped, "c", 1))
    summed = sums[0].astype(jnp.float32)
    for k in (1, 2, 3):
        summed = summed + shift(sums[k], "g", k).astype(jnp.float32)
    residual_sum = stream_here + summed
    squares = jnp.sum(residual_sum * residual_sum, axis=1)
    owner_dp = jnp.arange(64, dtype=jnp.int32) // 32
    outgoing = jnp.where((owner_dp == c)[:, None, None], squares[None, None], 0.0)
    arrived = lax.all_to_all(outgoing, PLANE, split_axis=0, concat_axis=0, tiled=True)
    residual = lax.ppermute(residual_sum.astype(jnp.bfloat16), PLANE, owner_pairs())
    total = jnp.sum(arrived, axis=(0, 1))
    scale = lax.rsqrt(total / D + 1e-06)[:, None]
    normed = residual.astype(jnp.float32) * scale * norm_gain.astype(jnp.float32)
    return (
        weight_new,
        moment_new,
        second_new,
        normed.astype(jnp.bfloat16),
        residual,
    )


def solution(mesh):
    torus = Mesh(mesh.devices.reshape(4, 2, 2, 8, 2), AXES)
    tensor = ("h", "z", "c")
    columns = ("d", "h", "z", "c")
    placed = (
        P("g", columns),
        P("g", columns),
        P("g", columns),
        P("g", columns),
        P(("g", "d"), tensor),
        P(("g", "d"), tensor),
        P(tensor),
    )
    return jax.shard_map(
        per_device,
        mesh=torus,
        in_specs=placed,
        out_specs=(
            P("g", columns),
            P("g", columns),
            P("g", columns),
            P(("g", "d"), tensor),
            P(("g", "d"), tensor),
        ),
        check_vma=False,
    )
```

```python
import math

import jax
import jax.numpy as jnp
from jax import lax
from jax.experimental import pallas as pl
from jax.experimental.pallas import tpu as pltpu
from jax.sharding import Mesh
from jax.sharding import PartitionSpec as P


D = 8192
FFW = 14848
AXES = ("g", "d", "h", "z", "c")
PLANE = ("d", "h", "z", "c")
SIZES = {"g": 4, "d": 2, "h": 2, "z": 8, "c": 2}
SLICE = 464

clip_rms = 0.5
beta_one = 0.9
beta_two = 0.95
bias_one = 1.0 - 0.9**10
bias_two = 1.0 - 0.95**10
adam_eps = 1e-08
learn_rate = 0.002


def shift(x, axis, k):
    n = SIZES[axis]
    return lax.ppermute(x, axis, [(i, (i + k) % n) for i in range(n)])


def shift_y(x, k):
    pairs = []
    for d in range(2):
        for h in range(2):
            y = (h * 2 + d + k) % 4
            pairs.append((d * 2 + h, (y % 2) * 2 + y // 2))
    return lax.ppermute(x, ("d", "h"), pairs)


def to_plane(x):
    pairs = []
    for g in range(4):
        for d in range(2):
            for h in range(2):
                for z in range(8):
                    for c in range(2):
                        src = (((g * 2 + d) * 2 + h) * 8 + z) * 2 + c
                        half, plane = z // 4, h * 2 + z // 4
                        y = (2 * h + d + 2 - (g - plane)) % 4
                        at_z = (4 * half - 2 + z % 4 * 2 + c) % 8
                        dst = (((plane * 2 + y % 2) * 2 + y // 2) * 8 + at_z) * 2 + d
                        pairs.append((src, dst))
    return lax.ppermute(x, AXES, pairs)


def owner_pairs():
    pairs = []
    for d in range(2):
        for h in range(2):
            for z in range(8):
                for c in range(2):
                    src = ((d * 2 + h) * 8 + z) * 2 + c
                    dst = ((c * 2 + d) * 8 + h * 4 + z // 2) * 2 + z % 2
                    pairs.append((src, dst))
    return pairs


VMEM = pl.BlockSpec(memory_space=pltpu.VMEM)
SMEM = pl.BlockSpec(memory_space=pltpu.SMEM)
ANY = pl.BlockSpec(memory_space=pltpu.HBM)


def packed(groups):
    flat = [x for group in groups for x in group]

    def kernel(*refs):
        sems, copies = refs[-1], []
        for out, group in zip(refs[len(flat) : -1], groups):
            for k in range(len(group)):
                n = len(copies)
                copies.append(pltpu.make_async_copy(refs[n], out.at[k], sems.at[n]))
        for copy in copies:
            copy.start()
        for copy in copies:
            copy.wait()

    return pl.pallas_call(
        kernel,
        out_shape=[
            jax.ShapeDtypeStruct((len(group), *group[0].shape), group[0].dtype)
            for group in groups
        ],
        in_specs=[ANY] * len(flat),
        out_specs=[VMEM] * len(groups),
        scratch_shapes=[pltpu.SemaphoreType.DMA((len(flat),))],
        compiler_params=pltpu.CompilerParams(vmem_limit_bytes=8 * 1024 * 1024),
        cost_estimate=pl.CostEstimate(flops=0, bytes_accessed=1_000_000, transcendentals=0),
    )(*flat)


def optimizer(factor, weight, moment, second, gradient):
    clipped = factor * gradient
    moment_new = beta_one * moment + (1.0 - beta_one) * clipped
    second_new = beta_two * second + (1.0 - beta_two) * clipped * clipped
    update = moment_new / bias_one / (jnp.sqrt(second_new / bias_two) + adam_eps)
    weight_new = weight - learn_rate * update
    return weight_new, moment_new, second_new, weight_new.astype(jnp.bfloat16)


def product(pieces, own, other, running, last):
    g, d, h, z, c = (lax.axis_index(a) for a in AXES)
    y = h * 2 + d
    first = 2 * (g >> 1) + c + 2 - y
    wheres = [((z - j - 4 * (g & 1) + 2) & 7) * SLICE for _, j, _ in pieces]
    owners = [(first + i) & 3 for i in range(4)]
    index = jnp.stack(wheres + owners + [c]).astype(jnp.int32)
    arrays = [array for _, _, array in pieces]
    many = len(arrays)
    acc = jax.ShapeDtypeStruct((4, 128, 256), jnp.float32)

    def kernel(index_ref, own_ref, other_ref, *refs):
        refs = list(refs)
        start_ref = refs.pop(0) if running is not None else None
        blocks, refs = refs[:many], refs[many:]
        outs, refs = (refs[:4], refs[4:]) if last else (None, refs)
        total, refs = refs[0], refs[1:]
        held, sems = refs[:many], refs[many]
        copies = [
            pltpu.make_async_copy(block, buffer, sems.at[k])
            for k, (block, buffer) in enumerate(zip(blocks, held))
        ]
        for copy in copies:
            copy.start()
        total[...] = jnp.zeros_like(total) if running is None else start_ref[...]
        for n, ((ys, _, _), copy, buffer) in enumerate(zip(pieces, copies, held)):
            copy.wait()
            at = pl.multiple_of(index_ref[n], 16)
            where = pl.ds(at, SLICE)
            weights = jnp.concatenate([own_ref[where, :], other_ref[where, :]], axis=1)
            for k, i in enumerate(ys):
                total[index_ref[many + i % 4]] += lax.dot_general(
                    buffer[k],
                    weights,
                    (((0,), (0,)), ((), ())),
                    preferred_element_type=jnp.float32,
                )
        if last:
            core = index_ref[many + 4]
            for side in range(2):
                where = pl.multiple_of((core if side == 0 else 1 - core) * 128, 128)
                for k in range(4):
                    part = total[k, :, side * 128 : (side + 1) * 128]
                    outs[k][:, pl.ds(where, 128)] = part.astype(jnp.bfloat16)

    return pl.pallas_call(
        kernel,
        out_shape=[jax.ShapeDtypeStruct((128, 256), jnp.bfloat16)] * 4 if last else acc,
        in_specs=[SMEM, VMEM, VMEM] + [VMEM] * (running is not None) + [ANY] * many,
        out_specs=[VMEM] * 4 if last else VMEM,
        scratch_shapes=([pltpu.VMEM(acc.shape, acc.dtype)] if last else [])
        + [pltpu.VMEM(array.shape, array.dtype) for array in arrays]
        + [pltpu.SemaphoreType.DMA((many,))],
        compiler_params=pltpu.CompilerParams(vmem_limit_bytes=12 * 1024 * 1024),
        cost_estimate=pl.CostEstimate(
            flops=sum(2 * array.size * 256 for array in arrays),
            bytes_accessed=sum(2 * array.size for array in arrays),
            transcendentals=0,
        ),
    )(index, own, other, *([] if running is None else [running]), *arrays)


def per_device(weight, moment, second, gradient, hidden, stream, norm_gain):
    c = lax.axis_index("c")
    mine = to_plane(hidden.T)
    y_one, y_back = shift_y(mine, 1), shift_y(mine, -1)
    y_two = shift_y(mine, 2)
    half_a, half_b = packed([[mine, y_one], [y_back, y_two]])
    ups_a, ups_b, downs_a, downs_b = [half_a], [half_b], [half_a], [half_b]
    for k in range(1, 5):
        ups_a.append(shift(ups_a[-1], "z", 1))
        if k < 4:
            downs_a.append(shift(downs_a[-1], "z", -1))
            ups_b.append(shift(ups_b[-1], "z", 1))
        downs_b.append(shift(downs_b[-1], "z", -1))

    grad_float = gradient.astype(jnp.float32)
    partial = jnp.sum(grad_float * grad_float, axis=0)[None, None]
    for axes in (("z", "c"), ("g", "d", "h")):
        spread = jnp.broadcast_to(partial, (16, 1, 128))
        reached = lax.all_to_all(spread, axes, split_axis=0, concat_axis=0, tiled=True)
        partial = jnp.sum(reached, axis=0, keepdims=True)
    grad_total = jnp.sum(partial)
    factor = jnp.minimum(1.0, clip_rms * math.sqrt(FFW * D) / (jnp.sqrt(grad_total) + 1e-06))
    weight_new, moment_new, second_new, shipped = optimizer(
        factor, weight, moment, second, grad_float
    )
    other = shift(shipped, "c", 1)
    from_owner = [(b, a) for a, b in owner_pairs()]
    stream_here = lax.ppermute(stream, PLANE, from_owner).astype(jnp.float32)

    y_a, y_b = (0, 1), (-1, 2)
    steps = [[(y_a, 0, half_a), (y_b, 0, half_b)]]
    for k in (1, 2, 3):
        steps.append([(y_a, k, ups_a[k]), (y_b, k, ups_b[k])])
        steps[-1] += [(y_a, -k, downs_a[k]), (y_b, -k, downs_b[k])]
    late = [(y_a, 4, ups_a[4]), (y_b, -4, downs_b[4])]
    running = product(steps[0] + steps[1], shipped, other, None, False)
    running = product(steps[2], shipped, other, running, False)
    running = product(steps[3], shipped, other, running, False)
    sums = product(late, shipped, other, running, True)
    summed = sums[0].astype(jnp.float32)
    for k in (2, 1, 3):
        summed = summed + shift(sums[k], "g", k).astype(jnp.float32)
    residual_sum = stream_here + summed
    residual = lax.ppermute(residual_sum.astype(jnp.bfloat16), PLANE, owner_pairs())
    row_squares = jnp.sum(residual_sum * residual_sum, axis=1)[None]
    theirs = shift(row_squares, "c", 1)
    owner_dp = jnp.arange(32, dtype=jnp.int32)[:, None, None] // 16
    outgoing = jnp.where(owner_dp == c, row_squares[None], theirs[None])
    arrived = lax.all_to_all(outgoing, ("d", "h", "z"), split_axis=0, concat_axis=0, tiled=True)
    total = jnp.sum(arrived, axis=(0, 1))
    scale = lax.rsqrt(total / D + 1e-06)[:, None]
    normed = residual.astype(jnp.float32) * scale * norm_gain.astype(jnp.float32)
    return (
        weight_new,
        moment_new,
        second_new,
        normed.astype(jnp.bfloat16),
        residual,
    )


def solution(mesh):
    torus = Mesh(mesh.devices.reshape(4, 2, 2, 8, 2), AXES)
    tensor = ("h", "z", "c")
    columns = ("d", "h", "z", "c")
    placed = (
        P("g", columns),
        P("g", columns),
        P("g", columns),
        P("g", columns),
        P(("g", "d"), tensor),
        P(("g", "d"), tensor),
        P(tensor),
    )

    return jax.shard_map(
        per_device,
        mesh=torus,
        in_specs=placed,
        out_specs=(
            P("g", columns),
            P("g", columns),
            P("g", columns),
            P(("g", "d"), tensor),
            P(("g", "d"), tensor),
        ),
        check_vma=False,
    )
```

```python
import math

import jax
import jax.numpy as jnp
from jax import lax
from jax.experimental import pallas as pl
from jax.experimental.pallas import tpu as pltpu
from jax.sharding import Mesh
from jax.sharding import PartitionSpec as P


D = 8192
FFW = 14848
AXES = ("g", "d", "h", "z", "c")
PLANE = ("d", "h", "z", "c")
SIZES = {"g": 4, "d": 2, "h": 2, "z": 8, "c": 2}
SLICE = 464

clip_rms = 0.5
beta_one = 0.9
beta_two = 0.95
bias_one = 1.0 - 0.9**10
bias_two = 1.0 - 0.95**10
adam_eps = 1e-08
learn_rate = 0.002


def shift(x, axis, k):
    n = SIZES[axis]
    return lax.ppermute(x, axis, [(i, (i + k) % n) for i in range(n)])


def shift_y(x, k):
    pairs = []
    for d in range(2):
        for h in range(2):
            y = (h * 2 + d + k) % 4
            pairs.append((d * 2 + h, (y % 2) * 2 + y // 2))
    return lax.ppermute(x, ("d", "h"), pairs)


def to_plane(x):
    pairs = []
    for g in range(4):
        for d in range(2):
            for h in range(2):
                for z in range(8):
                    for c in range(2):
                        src = (((g * 2 + d) * 2 + h) * 8 + z) * 2 + c
                        half, plane = z // 4, h * 2 + z // 4
                        y = (2 * h + d + 2 - (g - plane)) % 4
                        at_z = (4 * half - 2 + z % 4 * 2 + c) % 8
                        dst = (((plane * 2 + y % 2) * 2 + y // 2) * 8 + at_z) * 2 + d
                        pairs.append((src, dst))
    return lax.ppermute(x, AXES, pairs)


def owner_pairs():
    pairs = []
    for d in range(2):
        for h in range(2):
            for z in range(8):
                for c in range(2):
                    src = ((d * 2 + h) * 8 + z) * 2 + c
                    dst = ((c * 2 + d) * 8 + h * 4 + z // 2) * 2 + z % 2
                    pairs.append((src, dst))
    return pairs


VMEM = pl.BlockSpec(memory_space=pltpu.VMEM)
SMEM = pl.BlockSpec(memory_space=pltpu.SMEM)
ANY = pl.BlockSpec(memory_space=pltpu.HBM)


def packed(groups):
    flat = [x for group in groups for x in group]

    def kernel(*refs):
        sems, copies = refs[-1], []
        for out, group in zip(refs[len(flat) : -1], groups):
            for k in range(len(group)):
                n = len(copies)
                copies.append(pltpu.make_async_copy(refs[n], out.at[k], sems.at[n]))
        for copy in copies:
            copy.start()
        for copy in copies:
            copy.wait()

    return pl.pallas_call(
        kernel,
        out_shape=[
            jax.ShapeDtypeStruct((len(group), *group[0].shape), group[0].dtype)
            for group in groups
        ],
        in_specs=[ANY] * len(flat),
        out_specs=[VMEM] * len(groups),
        scratch_shapes=[pltpu.SemaphoreType.DMA((len(flat),))],
        compiler_params=pltpu.CompilerParams(vmem_limit_bytes=8 * 1024 * 1024),
        cost_estimate=pl.CostEstimate(flops=0, bytes_accessed=1_000_000, transcendentals=0),
    )(*flat)


def optimizer(factor, weight, moment, second, gradient):
    clipped = factor * gradient
    moment_new = beta_one * moment + (1.0 - beta_one) * clipped
    second_new = beta_two * second + (1.0 - beta_two) * clipped * clipped
    update = moment_new / bias_one / (jnp.sqrt(second_new / bias_two) + adam_eps)
    weight_new = weight - learn_rate * update
    return weight_new, moment_new, second_new, weight_new.astype(jnp.bfloat16)


def product(pieces, own, other, running, last):
    g, d, h, z, c = (lax.axis_index(a) for a in AXES)
    first = 2 * (g >> 1) + c + 2 - (h * 2 + d)
    wheres = [((z - j - 4 * (g & 1) + 2) & 7) * SLICE for _, j, _ in pieces]
    index = jnp.stack(wheres + [(k - first) & 3 for k in range(4)] + [c]).astype(jnp.int32)
    arrays = [array for _, _, array in pieces]
    many = len(arrays)
    acc = jax.ShapeDtypeStruct((4, 128, 256), jnp.float32)

    def kernel(index_ref, own_ref, other_ref, *refs):
        start_ref, refs = (None, refs) if running is None else (refs[0], refs[1:])
        blocks, outs = refs[:many], refs[many:]
        total = outs[-1]
        weights = {}
        for n, (_, j, _) in enumerate(pieces):
            if j % 8 not in weights:
                where = pl.ds(pl.multiple_of(index_ref[n], 16), SLICE)
                weights[j % 8] = jnp.concatenate([own_ref[where, :], other_ref[where, :]], axis=1)
        sums = {}
        for (ys, j, _), block in zip(pieces, blocks):
            for k, i in enumerate(ys):
                part = lax.dot_general(
                    block[k],
                    weights[j % 8],
                    (((0,), (0,)), ((), ())),
                    preferred_element_type=jnp.float32,
                )
                sums[i % 4] = part if i % 4 not in sums else sums[i % 4] + part
        for i in range(4):
            total[i] = sums[i] if running is None else start_ref[i] + sums[i]
        if last:
            core = index_ref[many + 4]
            for side in range(2):
                where = pl.multiple_of((core if side == 0 else 1 - core) * 128, 128)
                for k in range(4):
                    part = total[index_ref[many + k], :, side * 128 : (side + 1) * 128]
                    outs[k][:, pl.ds(where, 128)] = part.astype(jnp.bfloat16)

    return pl.pallas_call(
        kernel,
        out_shape=[jax.ShapeDtypeStruct((128, 256), jnp.bfloat16)] * 4 if last else acc,
        in_specs=[SMEM, VMEM, VMEM] + [VMEM] * (running is not None) + [VMEM] * many,
        out_specs=[VMEM] * 4 if last else VMEM,
        scratch_shapes=[pltpu.VMEM(acc.shape, acc.dtype)] if last else [],
        compiler_params=pltpu.CompilerParams(vmem_limit_bytes=12 * 1024 * 1024),
        cost_estimate=pl.CostEstimate(
            flops=sum(2 * array.size * 256 for array in arrays),
            bytes_accessed=sum(2 * array.size for array in arrays),
            transcendentals=0,
        ),
    )(index, own, other, *([] if running is None else [running]), *arrays)


def per_device(weight, moment, second, gradient, hidden, stream, norm_gain):
    c = lax.axis_index("c")
    mine = to_plane(hidden.T)
    y_one, y_back = shift_y(mine, 1), shift_y(mine, -1)
    y_two = shift_y(mine, 2)
    half_a, half_b = packed([[mine, y_one], [y_back, y_two]])
    ups_a, ups_b, downs_a, downs_b = [half_a], [half_b], [half_a], [half_b]
    for k in range(1, 5):
        ups_a.append(shift(ups_a[-1], "z", 1))
        if k < 4:
            downs_a.append(shift(downs_a[-1], "z", -1))
            ups_b.append(shift(ups_b[-1], "z", 1))
        downs_b.append(shift(downs_b[-1], "z", -1))

    grad_float = gradient.astype(jnp.float32)
    partial = jnp.sum(grad_float * grad_float, axis=0)[None, None]
    for axes in (("z", "c"), ("g", "d", "h")):
        spread = jnp.broadcast_to(partial, (16, 1, 128))
        reached = lax.all_to_all(spread, axes, split_axis=0, concat_axis=0, tiled=True)
        partial = jnp.sum(reached, axis=0, keepdims=True)
    grad_total = jnp.sum(partial)
    factor = jnp.minimum(1.0, clip_rms * math.sqrt(FFW * D) / (jnp.sqrt(grad_total) + 1e-06))
    weight_new, moment_new, second_new, shipped = optimizer(
        factor, weight, moment, second, grad_float
    )
    other = shift(shipped, "c", 1)
    from_owner = [(b, a) for a, b in owner_pairs()]
    stream_here = lax.ppermute(stream, PLANE, from_owner).astype(jnp.float32)

    y_a, y_b = (0, 1), (-1, 2)
    steps = [[(y_a, 0, half_a), (y_b, 0, half_b)]]
    for k in (1, 2, 3):
        steps.append([(y_a, k, ups_a[k]), (y_b, k, ups_b[k])])
        steps[-1] += [(y_a, -k, downs_a[k]), (y_b, -k, downs_b[k])]
    late = [(y_a, 4, ups_a[4]), (y_b, -4, downs_b[4])]
    running = product(steps[0] + steps[1], shipped, other, None, False)
    running = product(steps[2], shipped, other, running, False)
    running = product(steps[3], shipped, other, running, False)
    sums = product(late, shipped, other, running, True)
    summed = sums[0].astype(jnp.float32)
    for k in (2, 1, 3):
        summed = summed + shift(sums[k], "g", k).astype(jnp.float32)
    residual_sum = stream_here + summed
    residual = lax.ppermute(residual_sum.astype(jnp.bfloat16), PLANE, owner_pairs())
    row_squares = jnp.sum(residual_sum * residual_sum, axis=1)[None]
    theirs = shift(row_squares, "c", 1)
    owner_dp = jnp.arange(32, dtype=jnp.int32)[:, None, None] // 16
    outgoing = jnp.where(owner_dp == c, row_squares[None], theirs[None])
    arrived = lax.all_to_all(outgoing, ("d", "h", "z"), split_axis=0, concat_axis=0, tiled=True)
    total = jnp.sum(arrived, axis=(0, 1))
    scale = lax.rsqrt(total / D + 1e-06)[:, None]
    normed = residual.astype(jnp.float32) * scale * norm_gain.astype(jnp.float32)
    return (
        weight_new,
        moment_new,
        second_new,
        normed.astype(jnp.bfloat16),
        residual,
    )


def solution(mesh):
    torus = Mesh(mesh.devices.reshape(4, 2, 2, 8, 2), AXES)
    tensor = ("h", "z", "c")
    columns = ("d", "h", "z", "c")
    placed = (
        P("g", columns),
        P("g", columns),
        P("g", columns),
        P("g", columns),
        P(("g", "d"), tensor),
        P(("g", "d"), tensor),
        P(tensor),
    )

    return jax.shard_map(
        per_device,
        mesh=torus,
        in_specs=placed,
        out_specs=(
            P("g", columns),
            P("g", columns),
            P("g", columns),
            P(("g", "d"), tensor),
            P(("g", "d"), tensor),
        ),
        check_vma=False,
    )
```
